32 devices in a mesh: rep: 8 (over y, x, core), tp: 4 (over z).
Axes of the slice: x: 2, y: 2, z: 4, core: 2. Of those that a mesh axis runs over, the one named last changes fastest.
Arguments:
- context: bfloat16 [8, 3, 512, 2560], P('rep', None, 'tp'), may hold values from -6 to 6
- residual: bfloat16 [8, 3, 2560, 512], P('rep', None, 'tp'), may hold values from -6 to 6
- cotangent: bfloat16 [8, 3, 2560, 512], P('rep', None, 'tp'), may hold values from -6 to 6
- norm_gain: bfloat16 [2560], P('tp'), may hold values from 0.099609375 to 1.8984375
- weight: bfloat16 [8, 2560, 2560], P('rep', 'tp'), may hold values from -6 to 6
- momentum: bfloat16 [8, 2560, 2560], P('rep', 'tp'), may hold values from -4 to 4
- round_start: int32 [1], replicated, may hold values from 0 to 7
Outputs:
- weight_out: bfloat16 [8, 2560, 2560], P('rep', 'tp')
- momentum_out: bfloat16 [8, 2560, 2560], P('rep', 'tp')
The draws below stay inside these ranges and needn't reach their ends.
Inputs may be any that keep to these rules, and one draw needn't show every extreme that they name: Step s of the window averages with the replica whose index differs in bit number (round_start + s) mod log2(8).
All inputs are finite; a program needn't handle non-finite values.
Results may differ from the reference program's by a relative error of at most 0.015.
Values may be sent and summed in bfloat16 or wider, within the bound.
No kernel may reach another device: no remote copies, remote signals or barrier semaphores. Data moves between devices by JAX's collectives and lax.ppermute only.
A program may use at most 128 MiB of HBM per device.

```python
import jax
import jax.numpy as jnp
from jax import lax

D = 2560
HF = 2560
SEQ = 512
STEPS = 3
REPLICAS = 8
N_REP = 8


def levels(stream_key, extent, shards, smallest, top_value):
    factor_of = 1.0
    for axis_at, blocks in shards:
        heights = jax.random.uniform(jax.random.fold_in(jax.random.fold_in(stream_key, 6), axis_at), (blocks,), jnp.float32, smallest / len(shards), top_value / len(shards))
        factor_of = factor_of * jnp.repeat(jnp.exp(heights), extent[axis_at] // blocks).reshape((-1,) + (1,) * (len(extent) - 1 - axis_at))
    return factor_of


def gaussian(stream_key, shape, deviation, most, split=(), held_as=jnp.bfloat16):
    values = deviation * jax.random.normal(stream_key, shape, jnp.float32)
    if split:
        values = values * levels(stream_key, shape, split, -0.22, 0.18)
    return jnp.clip(values, -most, most).astype(held_as)


def setup_inputs(seed: int = 0) -> dict:
    streams_of = jax.random.split(jax.random.key(seed), 8)
    context = gaussian(streams_of[0], (REPLICAS, STEPS, SEQ, HF), 1.0, 6.0, ((0, 8), (2, 4)))
    residual = gaussian(streams_of[1], (REPLICAS, STEPS, D, SEQ), 1.0, 6.0, ((0, 8), (2, 4)))
    cotangent = gaussian(streams_of[2], (REPLICAS, STEPS, D, SEQ), 1.0, 6.0, ((0, 8), (2, 4)))
    norm_gain = jnp.clip(1.0 + 0.18 * jax.random.normal(streams_of[3], (D,), jnp.float32), 0.099609375, 1.8984375).astype(jnp.bfloat16)
    weight = gaussian(streams_of[4], (REPLICAS, D, HF), 1.0, 6.0, ((0, 8), (1, 4)))
    momentum = gaussian(streams_of[5], (REPLICAS, D, HF), 0.5, 4.0, ((0, 8), (1, 4)))
    round_start = jax.random.randint(streams_of[6], (1,), 0, N_REP).astype(jnp.int32)
    return {"context": context, "residual": residual, "cotangent": cotangent, "norm_gain": norm_gain, "weight": weight, "momentum": momentum, "round_start": round_start}


learn_rate = 0.5
beta_decay = 0.9
epsilon = 1e-05

def replica_update(operands):
    weight_now, moment_now, context_now, residual_now, cotangent_now, gain_now = operands
    out_scale = HF ** (-0.5)
    projected = jnp.dot(weight_now, context_now.T, preferred_element_type=jnp.float32) * out_scale
    hidden = residual_now.astype(jnp.float32) + projected
    inverse = lax.rsqrt(lax.optimization_barrier(jnp.mean(hidden * hidden, axis=0, keepdims=True)) + epsilon)
    weighted = cotangent_now.astype(jnp.float32) * gain_now.astype(jnp.float32)[:, None]
    cross_mean = lax.optimization_barrier(jnp.mean(weighted * hidden, axis=0, keepdims=True))
    grad_hidden = (inverse * weighted - hidden * inverse * inverse * inverse * cross_mean).astype(jnp.bfloat16)
    gradient = jnp.dot(grad_hidden, context_now, preferred_element_type=jnp.float32) * out_scale
    fresh_moment = (beta_decay * moment_now.astype(jnp.float32) + gradient).astype(jnp.bfloat16)
    fresh_weight = (weight_now.astype(jnp.float32) - learn_rate * fresh_moment.astype(jnp.float32)).astype(jnp.bfloat16)
    return (fresh_weight, fresh_moment)

def reference(context, residual, cotangent, norm_gain, weight, momentum, round_start):
    bit_count = N_REP.bit_length() - 1
    gains = jnp.broadcast_to(norm_gain, (N_REP, D))
    for section in range(STEPS):
        weight, momentum = lax.map(replica_update, (weight, momentum, context[:, section], residual[:, section], cotangent[:, section], gains))
        bit_pick = ((round_start[0] + section) % bit_count).astype(jnp.int32)
        partner = jnp.bitwise_xor(jnp.arange(N_REP, dtype=jnp.int32), jnp.left_shift(jnp.ones((), jnp.int32), bit_pick))
        weight = ((weight.astype(jnp.float32) + weight[partner].astype(jnp.float32)) * 0.5).astype(jnp.bfloat16)
        momentum = ((momentum.astype(jnp.float32) + momentum[partner].astype(jnp.float32)) * 0.5).astype(jnp.bfloat16)
    return (weight, momentum)
```

```python
from functools import partial

import jax
import jax.numpy as jnp
from jax import lax
from jax.sharding import PartitionSpec as P

learn_rate = 0.5
beta_decay = 0.9
epsilon = 1e-05
LINE = 8


f32 = jnp.float32
bf16 = jnp.bfloat16


def local_bits(mesh):
    axis = mesh.axis_names.index("rep")
    table = mesh.devices if axis == 0 else mesh.devices.T
    count = table.shape[0]
    found = set()
    for bit in range(count.bit_length() - 1):
        if all(
            tuple(table[r, c].coords) == tuple(table[r ^ 1 << bit, c].coords)
            for r in range(count)
            for c in range(table.shape[1])
        ):
            found.add(bit)
    return frozenset(found)


def mean2(a, b):
    return ((a.astype(f32) + b.astype(f32)) * 0.5).astype(bf16)


def swap(block, bit):
    count = lax.axis_size("rep")
    return lax.ppermute(block, "rep", [(r, r ^ 1 << bit) for r in range(count)])


def swap_all(pieces, bit):
    if lax.axis_size("tp") > LINE:
        return [None, swap(pieces[1], bit)]
    return [swap(piece, bit) for piece in pieces]


def side(bit):
    return (lax.axis_index("rep") >> bit) & 1


def half(block, which):
    rows = block.shape[0] // 2
    return lax.dynamic_slice_in_dim(block, which * rows, rows, 0)


def join(mine, theirs, which):
    first = which == 0
    return jnp.concatenate([jnp.where(first, mine, theirs), jnp.where(first, theirs, mine)], axis=0)


def spread(block, bits):
    if not bits:
        return block
    if len(bits) == 1:
        return mean2(block, swap(block, bits[0]))
    bit = bits[0]
    own = side(bit)
    kept = mean2(half(block, own), swap(half(block, 1 - own), bit))
    kept = spread(kept, bits[1:])
    return join(kept, swap(kept, bit), own)


def mean_over(block, bits, split=(), near=frozenset(), whole=False):
    if split:
        bit = split[0]
        own = side(bit)
        kept = mean_over(half(block, own), bits, split[1:], near, whole)
        return join(kept, swap(kept, bit), own)
    close = [b for b in bits if b in near]
    far = [b for b in bits if b not in near]
    if close and far:
        bit = close[0]
        own = side(bit)
        kept = mean2(half(block, own), swap(half(block, 1 - own), bit))
        kept = mean_over(kept, [b for b in bits if b != bit], (), near, whole)
        return join(kept, swap(kept, bit), own)
    if len(far) == 2 and whole:
        block = mean2(block, swap(block, far[1]))
        return mean2(block, swap(block, far[0]))
    return spread(block, close + far[::-1])


def place(pieces):
    count = lax.axis_size("tp")
    if count > LINE:
        return pieces[1]
    me = lax.axis_index("tp")
    rows = pieces[0].shape[0]
    whole = jnp.zeros((count * rows, pieces[0].shape[1]), pieces[0].dtype)
    for far, piece in enumerate(pieces):
        at = ((me - far) % count) * rows
        whole = lax.dynamic_update_slice(whole, piece, (at, 0))
    return whole


def collect(own):
    count = lax.axis_size("tp")
    me = lax.axis_index("tp")
    if count == 1:
        return [own]
    if count > LINE:
        return [own, lax.all_gather(own, "tp", axis=0, tiled=True)]
    found = [own] + [None] * (count - 1)
    found[1] = lax.ppermute(own, "tp", [(i, (i + 1) % count) for i in range(count)])
    if count > 2:
        found[-1] = lax.ppermute(own, "tp", [(i, (i - 1) % count) for i in range(count)])
    right, left = found[1], found[-1]
    rights, lefts = {1: right}, {1: left}
    for far in range(2, count - 1):
        rights[far] = right = lax.ppermute(right, "tp", [(i - 1, i) for i in range(far, count)])
        lefts[far] = left = lax.ppermute(left, "tp", [(i + 1, i) for i in range(count - far)])
    for far in range(2, count - 1):
        found[far] = jnp.where(me >= far, rights[far], lefts[count - far])
    return found


def rows_by_tokens(weight, tokens):
    return lax.dot_general(weight, tokens, (((1,), (1,)), ((), ())), preferred_element_type=f32)


def by_tokens(grad_hidden, tokens):
    return jnp.dot(grad_hidden, tokens, preferred_element_type=f32)


def hidden_gradient(projected, residual, cotangent, gain_values, width):
    hidden = residual.astype(f32) + projected
    weighted = cotangent.astype(f32) * gain_values
    square_sum, cross_sum = lax.psum(
        (
            jnp.sum(hidden * hidden, axis=0, keepdims=True),
            jnp.sum(weighted * hidden, axis=0, keepdims=True),
        ),
        "tp",
    )
    inverse = lax.rsqrt(square_sum / width + epsilon)
    cross_mean = cross_sum / width
    return (inverse * weighted - hidden * inverse * inverse * inverse * cross_mean).astype(bf16)


def window(context, residual, cotangent, gain_values, weight, momentum, order, near):
    first, second, third = order
    out_scale = context.shape[-1] ** -0.5
    width = weight.shape[0] * lax.axis_size("tp")

    near_first, near_second, near_third = (b in near for b in order)

    pieces = [collect(context[0])]
    for s in (1, 2):
        own, pieces[-1] = lax.optimization_barrier((context[s], pieces[-1]))
        pieces.append(collect(own))
    tokens = [place(p) for p in pieces]

    def gradient_of(projected, s):
        return hidden_gradient(projected, residual[s], cotangent[s], gain_values, width)

    def pair_gradient(grad_hidden, s, bit):
        if bit in near:
            own = (by_tokens(grad_hidden, tokens[s]) * out_scale).astype(bf16)
            return mean2(own, swap(own, bit))
        peer_tokens = place(swap_all(pieces[s], bit))
        peer_hidden = swap(grad_hidden, bit)
        own = by_tokens(grad_hidden, tokens[s])
        return ((own + by_tokens(peer_hidden, peer_tokens)) * (0.5 * out_scale)).astype(bf16)

    projected = rows_by_tokens(weight, tokens[0]) * out_scale
    gradient = by_tokens(gradient_of(projected, 0), tokens[0]) * out_scale
    moment = (beta_decay * momentum.astype(f32) + gradient).astype(bf16)
    fresh = (weight.astype(f32) - learn_rate * moment.astype(f32)).astype(bf16)

    if near_first:
        fresh, moment = mean2(fresh, swap(fresh, first)), mean2(moment, swap(moment, first))
        projected = rows_by_tokens(fresh, tokens[1]) * out_scale
        split, rest = (first,), []
    else:
        peer_tokens = place(swap_all(pieces[1], first))
        for_peer = (rows_by_tokens(fresh, peer_tokens) * (0.5 * out_scale)).astype(bf16)
        projected = rows_by_tokens(fresh, tokens[1]) * (0.5 * out_scale) + swap(
            for_peer, first
        ).astype(f32)
        split, rest = (), [first]
    grad_one = pair_gradient(gradient_of(projected, 1), 1, second)

    ahead = (fresh.astype(f32) - learn_rate * beta_decay * moment.astype(f32)).astype(bf16)
    ahead = mean_over(ahead, rest + [second], split, near)
    moment_all = mean_over(moment, rest + [second, third], split, near, True)

    weight_two = (ahead.astype(f32) - learn_rate * grad_one.astype(f32)).astype(bf16)
    projected = rows_by_tokens(weight_two, tokens[2]) * out_scale
    grad_two = pair_gradient(gradient_of(projected, 2), 2, third).astype(f32)

    close = () if near_third else tuple(b for b in (first, second) if b in near)
    ahead_all = mean_over(ahead, [third], close, near).astype(f32)
    grad_one_all = mean_over(grad_one, [third], () if near_third else (second,), near).astype(f32)
    moment_all = moment_all.astype(f32)

    square = beta_decay * beta_decay
    moment_out = square * moment_all + beta_decay * grad_one_all + grad_two
    weight_out = (
        ahead_all
        - learn_rate * square * moment_all
        - (learn_rate + learn_rate * beta_decay) * grad_one_all
        - learn_rate * grad_two
    )
    return weight_out.astype(bf16), moment_out.astype(bf16)


def on_device(context, residual, cotangent, norm_gain, weight, momentum, round_start, near):
    bit_count = lax.axis_size("rep").bit_length() - 1
    gain_values = norm_gain.astype(f32)[:, None]
    branches = [
        partial(window, order=tuple((start + s) % bit_count for s in range(3)), near=near)
        for start in range(bit_count)
    ]
    weight_now, moment_now = lax.switch(
        round_start[0] % bit_count,
        branches,
        context[0],
        residual[0],
        cotangent[0],
        gain_values,
        weight[0],
        momentum[0],
    )
    return (weight_now[None], moment_now[None])


def solution(mesh):
    return jax.shard_map(
        partial(on_device, near=local_bits(mesh)),
        mesh=mesh,
        in_specs=(
            P("rep", None, "tp", None),
            P("rep", None, "tp", None),
            P("rep", None, "tp", None),
            P("tp"),
            P("rep", "tp", None),
            P("rep", "tp", None),
            P(),
        ),
        out_specs=(P("rep", "tp", None), P("rep", "tp", None)),
        check_vma=False,
    )
```
